256 devices in a mesh: batch: 4 (over y), lat: 8 (over x, core), lon: 8 (over z).
Axes of the slice: x: 4, y: 4, z: 8, core: 2. Of those that a mesh axis runs over, the one named last changes fastest.
Arguments:
- patches: bfloat16 [4, 16, 24, 128, 640], P('batch', 'lat', 'lon'), may hold values from -6 to 6
- kept_index: int32 [4, 16, 24, 64], P('batch', 'lat', 'lon'), may hold values from 0 to 127, as said below
- kept_count: int32 [4, 16, 24], P('batch', 'lat', 'lon'), may hold values from 32 to 64, as said below
- embed_weight: bfloat16 [640, 1280], P('batch'), may hold values from -0.25 to 0.25
- local_qkv: bfloat16 [1280, 3840], P('batch'), may hold values from -6 to 6
- local_out: bfloat16 [1280, 1280], P('batch'), may hold values from -0.15625 to 0.15625
- global_qkv: bfloat16 [1280, 3840], P('batch'), may hold values from -6 to 6
Outputs:
- mixed: bfloat16 [4, 16, 24, 64, 1280], P('batch', 'lat', 'lon')
The draws below stay inside these ranges and needn't reach their ends.
Inputs may be any that keep to these rules, and one draw needn't show every extreme that they name: `kept_index`: in each window all 64 entries are distinct offsets; the first kept_count of them are the kept tokens in rising order. `kept_count`: every device holds, in its sample, a window with exactly 64 kept tokens.
All inputs are finite; a program needn't handle non-finite values.
Results may differ from the reference program's by a relative error of at most 0.023.
Values may be sent and summed in bfloat16 or wider, within the bound.
A program may use at most 128 MiB of HBM per device.

```python
import jax
import jax.numpy as jnp
from jax import lax

PIN = 640
D = 1280
HEADS = 8
HD = 160
INNER = 1280
WT = 128
KMAX = 64
WLAT = 2
WLON = 3
SAMPLES = 4
NWLAT = 16
NWLON = 24


def kept_counts(key):
    base = jax.random.fold_in(key, 17)
    counts = jax.random.randint(base, (SAMPLES, NWLAT, NWLON), KMAX // 2, KMAX + 1)
    lat_first = (jnp.arange(NWLAT) % WLAT == 0)[None, :, None]
    lon_first = (jnp.arange(NWLON) % WLON == 0)[None, None, :]
    return jnp.where(lat_first & lon_first, KMAX, counts).astype(jnp.int32)


def draw_kept_count(key, part):
    return kept_counts(key)


def shuffle(sub_key):
    return jax.random.permutation(sub_key, WT)


def draw_kept_index(key, part):
    counts = kept_counts(key)
    total_windows = SAMPLES * NWLAT * NWLON
    sub_keys = jax.random.split(jax.random.fold_in(key, 29), total_windows)
    orders = jax.vmap(shuffle)(sub_keys).astype(jnp.int32)
    positions = jnp.arange(WT, dtype=jnp.int32)[None, :]
    chosen = positions < counts.reshape(total_windows, 1)
    ranked = jnp.sort(jnp.where(chosen, orders, orders + WT), axis=1)
    ranked = jnp.where(ranked >= WT, ranked - WT, ranked)
    return ranked[:, :KMAX].reshape(SAMPLES, NWLAT, NWLON, KMAX).astype(jnp.int32)


def drawn_qkv(key):
    base = jax.random.normal(jax.random.fold_in(key, 3), (D, 3, INNER), jnp.float32) * D ** (-0.5)
    base = jnp.clip(base, -6.0, 6.0)
    return base.reshape(D, 3 * INNER).astype(jnp.bfloat16)


def draw_local_qkv(key, part):
    return drawn_qkv(jax.random.fold_in(key, 41))


def draw_global_qkv(key, part):
    return drawn_qkv(jax.random.fold_in(key, 43))


def block_scale(own_key, dims, pieces, smallest, high):
    factor_of = 1.0
    for axis_at, parts in pieces:
        steps = jax.random.uniform(jax.random.fold_in(jax.random.fold_in(own_key, 6), axis_at), (parts,), jnp.float32, smallest / len(pieces), high / len(pieces))
        factor_of = factor_of * jnp.repeat(jnp.exp(steps), dims[axis_at] // parts).reshape((-1,) + (1,) * (len(dims) - 1 - axis_at))
    return factor_of


def noise(own_key, dims, scale, most, cuts=(), kind=jnp.bfloat16):
    drawn = scale * jax.random.normal(own_key, dims, jnp.float32)
    if cuts:
        drawn = drawn * block_scale(own_key, dims, cuts, -0.22, 0.18)
    return jnp.clip(drawn, -most, most).astype(kind)


def setup_inputs(seed: int = 0) -> dict:
    arg_keys = jax.random.split(jax.random.key(seed), 8)
    return {
        "patches": noise(arg_keys[0], (SAMPLES, NWLAT, NWLON, WT, PIN), 1.0, 6.0, ((0, 4), (1, 8), (2, 8))),
        "kept_index": draw_kept_index(jax.random.fold_in(arg_keys[7], 71), 0),
        "kept_count": draw_kept_count(jax.random.fold_in(arg_keys[7], 71), 0),
        "embed_weight": noise(arg_keys[3], (PIN, D), PIN ** -0.5, 0.25, ((0, 4),)),
        "local_qkv": draw_local_qkv(jax.random.fold_in(arg_keys[7], 71), 0),
        "local_out": noise(arg_keys[5], (INNER, D), INNER ** -0.5, 0.15625, ((0, 4),)),
        "global_qkv": draw_global_qkv(jax.random.fold_in(arg_keys[7], 71), 0),
    }


norm_eps = 1e-05
mask_floor = -1e+30

def rounded(values):
    return lax.optimization_barrier(values.astype(jnp.bfloat16))

def layer_norm(values):
    centre = values - lax.optimization_barrier(jnp.mean(values, axis=-1, keepdims=True))
    spread = lax.optimization_barrier(jnp.mean(centre * centre, axis=-1, keepdims=True))
    return centre * lax.rsqrt(spread + norm_eps)

def attend(query_rows, key_rows, value_rows, keep_mask):
    scores = jnp.einsum('bnhd,bmhd->bhnm', query_rows.astype(jnp.float32), key_rows.astype(jnp.float32)) * HD ** (-0.5)
    scores = jnp.where(keep_mask[:, None, None, :], scores, mask_floor)
    scores = scores - lax.optimization_barrier(jnp.max(scores, axis=-1, keepdims=True))
    weights = jnp.exp(scores)
    probabilities = rounded(weights / lax.optimization_barrier(jnp.sum(weights, axis=-1, keepdims=True)))
    blended = jnp.einsum('bhnm,bmhd->bnhd', probabilities.astype(jnp.float32), value_rows.astype(jnp.float32))
    return rounded(blended).reshape(query_rows.shape[0], query_rows.shape[1], HEADS * HD)

def reference(patches, kept_index, kept_count, embed_weight, local_qkv, local_out, global_qkv):

    def one_sample(inputs):
        patch_all, index_all, count_all = inputs
        windows = NWLAT * NWLON
        patch_rows = patch_all.reshape(windows, WT, PIN)
        index_rows = index_all.reshape(windows, KMAX)
        kept_mask = jnp.arange(KMAX, dtype=jnp.int32)[None, :] < count_all.reshape(windows, 1)
        picked = jnp.take_along_axis(patch_rows, index_rows[:, :, None], axis=1).reshape(windows * KMAX, PIN)
        embedded = rounded(jnp.dot(picked, embed_weight, preferred_element_type=jnp.float32))
        normed = rounded(layer_norm(embedded.astype(jnp.float32)))
        local_proj = rounded(jnp.dot(normed, local_qkv, preferred_element_type=jnp.float32))
        local_proj = local_proj.reshape(windows, KMAX, 3, HEADS, HD)
        local_mix = attend(local_proj[:, :, 0], local_proj[:, :, 1], local_proj[:, :, 2], kept_mask)
        local_mix = local_mix.reshape(windows * KMAX, HEADS * HD)
        hidden = rounded(embedded.astype(jnp.float32) + jnp.dot(local_mix, local_out, preferred_element_type=jnp.float32))
        normed_global = rounded(layer_norm(hidden.astype(jnp.float32)))
        global_proj = rounded(jnp.dot(normed_global, global_qkv, preferred_element_type=jnp.float32))
        global_proj = global_proj.reshape(windows, KMAX, 3 * HEADS * HD)
        window_ids = jnp.broadcast_to(jnp.arange(windows, dtype=jnp.int32)[:, None], (windows, KMAX))
        slot_rows = jnp.zeros((WT, windows, 3 * HEADS * HD), global_proj.dtype).at[index_rows, window_ids].set(global_proj)
        slot_keep = jnp.zeros((WT, windows), bool).at[index_rows, window_ids].set(kept_mask)
        block_rows = slot_rows.reshape(WT // 8, 8, windows, 3, HEADS, HD)
        block_keep = slot_keep.reshape(WT // 8, 8, windows)

        def offset_block(pair):
            rows_here, keep_here = pair
            return attend(rows_here[:, :, 0], rows_here[:, :, 1], rows_here[:, :, 2], keep_here)
        blended = lax.map(offset_block, (block_rows, block_keep)).reshape(WT, windows, HEADS * HD)
        gathered = blended[index_rows, window_ids]
        result = jnp.where(kept_mask[:, :, None], gathered, jnp.zeros_like(gathered))
        return result.reshape(NWLAT, NWLON, KMAX, HEADS * HD)
    return lax.map(one_sample, (patches, kept_index, kept_count))
```

```python
import jax
import jax.numpy as jnp
from jax import lax
from jax.sharding import PartitionSpec as P

HEADS = 8
HD = 160


norm_eps = 1e-05
mask_floor = -1e30


def layer_norm(values):
    centre = values - jnp.mean(values, axis=-1, keepdims=True)
    spread = jnp.mean(centre * centre, axis=-1, keepdims=True)
    return centre * lax.rsqrt(spread + norm_eps)


def product(left_rows, right_rows):
    return jnp.dot(left_rows, right_rows, preferred_element_type=jnp.float32)


def gather_weight(shard):
    rows = shard.shape[0] // lax.axis_size("lat")
    piece = lax.dynamic_slice_in_dim(shard, lax.axis_index("lat") * rows, rows, 0)
    return lax.all_gather(piece, ("batch", "lat"), axis=0, tiled=True)


def attend(proj, keep_mask):
    groups, rows = proj.shape[:2]
    split = proj.reshape(groups, rows, 3, HEADS, HD)
    scores = jnp.einsum(
        "bnhd,bmhd->bhnm", split[:, :, 0], split[:, :, 1], preferred_element_type=jnp.float32
    ) * HD ** (-0.5)
    scores = jnp.where(keep_mask[:, None, None, :], scores, mask_floor)
    scores = scores - jnp.max(scores, axis=-1, keepdims=True)
    weights = jnp.exp(scores)
    probabilities = (weights / jnp.sum(weights, axis=-1, keepdims=True)).astype(jnp.bfloat16)
    blended = jnp.einsum(
        "bhnm,bmhd->bnhd", probabilities, split[:, :, 2], preferred_element_type=jnp.float32
    )
    return blended.astype(jnp.bfloat16).reshape(groups, rows, HEADS * HD)


def body(patches, kept_index, kept_count, embed_weight, local_qkv, local_out, global_qkv):
    lat_windows = patches.shape[1]
    lon_windows = patches.shape[2]
    windows = lat_windows * lon_windows
    tokens = patches.shape[3]
    most = kept_index.shape[3]
    rows = windows * most
    inner = HEADS * HD
    owners = lax.axis_size("lat") * lax.axis_size("lon")
    owned = tokens // owners
    me = lax.axis_index("lat") * lax.axis_size("lon") + lax.axis_index("lon")

    patch_rows = patches.reshape(windows, tokens, patches.shape[4])
    kept = lax.broadcasted_iota(jnp.int32, (windows, most), 1) < kept_count.reshape(windows, 1)
    marks = jnp.where(kept, kept_index.reshape(windows, most), -1)
    all_marks = lax.all_gather(marks, ("lat", "lon"), axis=0, tiled=True)
    wanted = me + owners * lax.broadcasted_iota(jnp.int32, (owned, 1, 1), 0)
    member = jnp.any(all_marks[None] == wanted, axis=-1)

    chosen = (
        marks[:, :, None] == lax.broadcasted_iota(jnp.int32, (windows, most, tokens), 2)
    ).astype(jnp.bfloat16)
    picked = jnp.einsum(
        "wkt,wtd->wkd", chosen, patch_rows, preferred_element_type=jnp.float32
    ).astype(jnp.bfloat16).reshape(rows, -1)
    embedded = product(picked, gather_weight(embed_weight)).astype(jnp.bfloat16)
    normed = layer_norm(embedded.astype(jnp.float32)).astype(jnp.bfloat16)
    local_proj = product(normed, gather_weight(local_qkv)).astype(jnp.bfloat16)
    local_mix = attend(local_proj.reshape(windows, most, -1), kept).reshape(rows, inner)
    hidden = (
        embedded.astype(jnp.float32) + product(local_mix, gather_weight(local_out))
    ).astype(jnp.bfloat16)
    normed_global = layer_norm(hidden.astype(jnp.float32)).astype(jnp.bfloat16)
    slots = jnp.einsum(
        "wkt,wkd->twd",
        chosen,
        normed_global.reshape(windows, most, -1),
        preferred_element_type=jnp.float32,
    ).astype(jnp.bfloat16)
    received = lax.all_to_all(
        slots.reshape(owned, owners, windows, -1),
        ("lat", "lon"),
        split_axis=1,
        concat_axis=1,
        tiled=True,
    )
    group = owners * windows
    global_proj = product(received.reshape(owned * group, -1), gather_weight(global_qkv))
    blended = attend(
        global_proj.astype(jnp.bfloat16).reshape(owned, group, -1), member.reshape(owned, group)
    )
    returned = lax.all_to_all(
        blended.reshape(owned, owners, windows, inner),
        ("lat", "lon"),
        split_axis=1,
        concat_axis=1,
        tiled=True,
    ).reshape(tokens, windows, inner)
    result = jnp.einsum(
        "wkt,twd->wkd", chosen, returned, preferred_element_type=jnp.float32
    ).astype(jnp.bfloat16)
    return result.reshape(1, lat_windows, lon_windows, most, inner)


def solution(mesh):
    return jax.shard_map(
        body,
        mesh=mesh,
        in_specs=(
            P("batch", "lat", "lon", None, None),
            P("batch", "lat", "lon", None),
            P("batch", "lat", "lon"),
            P("batch", None),
            P("batch", None),
            P("batch", None),
            P("batch", None),
        ),
        out_specs=P("batch", "lat", "lon", None, None),
        check_vma=False,
    )
```
